32 devices in a mesh: cell: 16 (over z, y, x), win: 2 (over core).
Axes of the slice: x: 2, y: 2, z: 4, core: 2. Of those that a mesh axis runs over, the one named last changes fastest.
Arguments:
- anomalies: bfloat16 [256, 60, 8192], P('win', None, 'cell'), may hold values from -6 to 6
- eofs: bfloat16 [100, 60, 8192], P('win', None, 'cell'), may hold values from -0.015625 to 0.015625
- cell_area: float32 [8192], P('cell'), may hold values from 0.5 to 2
- levels: int32 [8192], P('cell'), may hold values from 1 to 60
- counts: int32 [16], replicated, may hold values from 128 to 512, as said below
Outputs:
- pcs: float32 [256, 100], P('win')
- regression: float32 [100, 8192], P('win', 'cell')
The draws below stay inside these ranges and needn't reach their ends.
Inputs may be any that keep to these rules, and one draw needn't show every extreme that they name: `counts`: every entry is at most 512, and some block holds exactly 512 real cells.
All inputs are finite; a program needn't handle non-finite values.
Results may differ from the reference program's by a relative error of at most 0.0049.
Values may be sent and summed in bfloat16 or wider, within the bound.
No kernel may reach another device: no remote copies, remote signals or barrier semaphores. Data moves between devices by JAX's collectives and lax.ppermute only.
A program may use at most 64 MiB of HBM per device.

```python
import math
import jax
import jax.numpy as jnp
from jax import lax

K = 100
LEVELS = 60
CAP = 512
CELLS = 8192
TIMES = 256
N_CELL = 16


def draw_counts(key, part):
    values = jax.random.randint(key, (N_CELL,), CAP // 4, CAP + 1)
    where = jax.random.randint(jax.random.fold_in(key, 7), (), 0, N_CELL)
    return values.at[where].set(CAP).astype(jnp.int32)


def with_ends(drawn, key, least, high):
    dims = drawn.shape
    spot = [jax.random.randint(jax.random.fold_in(key, axis), (), 0, dims[axis]) for axis in range(len(dims))]
    drawn = drawn.at[tuple(spot)].set(least)
    longest = dims.index(max(dims))
    spot[longest] = (spot[longest] + 1) % dims[longest]
    return drawn.at[tuple(spot)].set(high)


def steps_of(key, dims, cuts, smallest, largest):
    gain = 1.0
    for position, shards_of in cuts:
        heights = jax.random.uniform(jax.random.fold_in(jax.random.fold_in(key, 6), position), (shards_of,), jnp.float32, smallest / len(cuts), largest / len(cuts))
        gain = gain * jnp.repeat(jnp.exp(heights), dims[position] // shards_of).reshape((-1,) + (1,) * (len(dims) - 1 - position))
    return gain


def noise(rng, extent, spread, most, shards=(), held_as=jnp.bfloat16):
    gain = steps_of(rng, extent, shards, -0.22, 0.18) if shards else 1.0
    values = jax.random.normal(rng, extent, jnp.float32) * spread * gain
    return jnp.minimum(jnp.maximum(values, -most), most).astype(held_as)


def setup_inputs(seed: int = 0) -> dict:
    key_list = jax.random.split(jax.random.key(seed), 6)
    anomalies = noise(key_list[0], (TIMES, LEVELS, CELLS), 1.0, 6.0, ((0, 2), (2, 16)))
    eofs = noise(key_list[1], (K, LEVELS, CELLS), (LEVELS * CELLS // 4) ** -0.5, 0.015625, ((0, 2), (2, 16)))
    cell_area = jnp.clip(jnp.exp(math.log(2.0) - 1.3862944 * jax.random.uniform(key_list[2], (CELLS,), jnp.float32) ** steps_of(key_list[2], (CELLS,), ((0, 16),), -0.2, 0.2)), 0.5, 2.0)
    levels = with_ends(jax.random.randint(key_list[3], (CELLS,), 1, LEVELS + 1), jax.random.fold_in(key_list[3], 1), 1, LEVELS).astype(jnp.int32)
    counts = draw_counts(jax.random.fold_in(key_list[5], 71), 0)
    return dict(anomalies=anomalies, eofs=eofs, cell_area=cell_area, levels=levels, counts=counts)


def reference(anomalies, eofs, cell_area, levels, counts):
    slot = jnp.arange(CELLS, dtype=jnp.int32)
    owner = slot // CAP
    live = slot % CAP < counts[owner]
    depth = jnp.arange(LEVELS, dtype=jnp.int32)[:, None] < levels[None, :]
    mask = (live[None, :] & depth).astype(jnp.float32)
    weighted = (eofs.astype(jnp.float32) * (cell_area[None, :] * mask)[None]).astype(jnp.bfloat16)
    flat_data = anomalies.reshape(TIMES, LEVELS * CELLS)
    flat_eofs = weighted.reshape(K, LEVELS * CELLS)
    pcs = lax.dot_general(flat_data, flat_eofs, (((1,), (1,)), ((), ())), preferred_element_type=jnp.float32)
    column = lax.optimization_barrier(jnp.sum(anomalies.astype(jnp.float32) * mask[None], axis=1)).astype(jnp.bfloat16)
    pcs_rounded = pcs.astype(jnp.bfloat16)
    regression = lax.dot_general(pcs_rounded, column, (((0,), (0,)), ((), ())), preferred_element_type=jnp.float32)
    regression = regression / jnp.sqrt(jnp.float32(TIMES))
    return (pcs, regression)
```

```python
import jax
import jax.numpy as jnp
from jax import lax
from jax.sharding import PartitionSpec as P


def exchange_sum(value, size):
    step = 1
    while step < size:
        if size % (4 * step) == 0:
            far, side, near = [
                lax.ppermute(value, "cell", [(i, i ^ k) for i in range(size)]) for k in (3 * step, 2 * step, step)
            ]
            value = (value + near) + (side + far)
            step *= 4
        else:
            value = value + lax.ppermute(value, "cell", [(i, i ^ step) for i in range(size)])
            step *= 2
    return value


def sum_cells(value, size):
    if size & (size - 1):
        return lax.psum(value, "cell")
    return exchange_sum(value, size)


def swap(value):
    return lax.ppermute(value, "win", [(0, 1), (1, 0)])


def make(cells):
    def shards(anomalies, eofs, cell_area, levels, counts):
        steps_here, depth_count, slots = anomalies.shape
        own = eofs.shape[0]
        filled = counts[lax.axis_index("cell")]
        window = lax.axis_index("win")
        other_eofs = swap(eofs)
        live = jnp.arange(slots, dtype=jnp.int32) < filled
        depth = jnp.arange(depth_count, dtype=jnp.int32)[:, None] < levels[None, :]
        mask = (live[None, :] & depth).astype(jnp.float32)
        scale = (cell_area[None, :] * mask)[None]
        column = jnp.sum(anomalies.astype(jnp.float32) * mask[None], axis=1).astype(jnp.bfloat16)
        other_column = swap(column)
        flat = anomalies.reshape(steps_here, depth_count * slots)

        def project(patterns):
            weighted = (patterns.astype(jnp.float32) * scale).astype(jnp.bfloat16)
            return lax.dot_general(
                flat, weighted.reshape(own, depth_count * slots), (((1,), (1,)), ((), ())), preferred_element_type=jnp.float32
            )

        total = sum_cells(jnp.concatenate([project(eofs), project(other_eofs)], axis=1), cells)
        mine, others = total[:, :own], total[:, own:]
        pcs = jnp.where(window == 0, total, jnp.concatenate([others, mine], axis=1))
        arrived = swap(others.astype(jnp.bfloat16))
        terms = lax.dot_general(
            mine.astype(jnp.bfloat16), column, (((0,), (0,)), ((), ())), preferred_element_type=jnp.float32
        ) + lax.dot_general(arrived, other_column, (((0,), (0,)), ((), ())), preferred_element_type=jnp.float32)
        return pcs, terms / jnp.sqrt(jnp.float32(steps_here * 2))

    return shards


def solution(mesh):
    in_specs = (P("win", None, "cell"), P("win", None, "cell"), P("cell"), P("cell"), P())
    out_specs = (P("win", None), P("win", "cell"))
    return jax.shard_map(
        make(mesh.shape["cell"]), mesh=mesh, in_specs=in_specs, out_specs=out_specs, check_vma=False
    )
```
